32 devices in a mesh: fsdp: 16 (over z, x, core), seq: 2 (over y).
Axes of the slice: x: 2, y: 2, z: 4, core: 2. Of those that a mesh axis runs over, the one named last changes fastest.
Arguments:
- inputs: bfloat16 [64, 1104, 512], P('fsdp', 'seq'), may hold values from -6 to 6
- skip_input: bfloat16 [64, 1104, 512], P('fsdp', 'seq'), may hold values from -6 to 6
- cotangent: bfloat16 [64, 1104, 512], P('fsdp', 'seq'), may hold values from -6 to 6
- text_len: int32 [64], P('fsdp'), may hold values from 1 to 79, as said below
- batch_valid: int32 [16, 4], P('fsdp'), may hold values 0 or 1
- skip_weight: bfloat16 [1024, 512], P(('fsdp', 'seq')), may hold values from -0.1875 to 0.1875
- skip_bias: bfloat16 [512], P(('fsdp', 'seq')), may hold values from -3 to 3
- first_gain: bfloat16 [512], P(('fsdp', 'seq')), may hold values from 0.099609375 to 1.8984375
- first_shift: bfloat16 [512], P(('fsdp', 'seq')), may hold values from -3 to 3
- qkv_weight: bfloat16 [512, 1536], P(('fsdp', 'seq')), may hold values from -0.25 to 0.25
- proj_weight: bfloat16 [512, 512], P(('fsdp', 'seq')), may hold values from -3 to 3
- proj_bias: bfloat16 [512], P(('fsdp', 'seq')), may hold values from -3 to 3
- second_gain: bfloat16 [512], P(('fsdp', 'seq')), may hold values from 0.099609375 to 1.8984375
- second_shift: bfloat16 [512], P(('fsdp', 'seq')), may hold values from -3 to 3
- up_weight: bfloat16 [512, 2048], P(('fsdp', 'seq')), may hold values from -0.25 to 0.25
- up_bias: bfloat16 [2048], P(('fsdp', 'seq')), may hold values from -3 to 3
- down_weight: bfloat16 [2048, 512], P(('fsdp', 'seq')), may hold values from -0.125 to 0.125
- down_bias: bfloat16 [512], P(('fsdp', 'seq')), may hold values from -3 to 3
Outputs:
- output: bfloat16 [64, 1104, 512], P('fsdp', 'seq')
- input_grad: bfloat16 [64, 1104, 512], P('fsdp', 'seq')
- skip_grad: bfloat16 [64, 1104, 512], P('fsdp', 'seq')
- skip_weight_grad: float32 [1024, 512], P(('fsdp', 'seq'))
- skip_bias_grad: float32 [512], P(('fsdp', 'seq'))
- first_gain_grad: float32 [512], P(('fsdp', 'seq'))
- first_shift_grad: float32 [512], P(('fsdp', 'seq'))
- qkv_weight_grad: float32 [512, 1536], P(('fsdp', 'seq'))
- proj_weight_grad: float32 [512, 512], P(('fsdp', 'seq'))
- proj_bias_grad: float32 [512], P(('fsdp', 'seq'))
- second_gain_grad: float32 [512], P(('fsdp', 'seq'))
- second_shift_grad: float32 [512], P(('fsdp', 'seq'))
- up_weight_grad: float32 [512, 2048], P(('fsdp', 'seq'))
- up_bias_grad: float32 [2048], P(('fsdp', 'seq'))
- down_weight_grad: float32 [2048, 512], P(('fsdp', 'seq'))
- down_bias_grad: float32 [512], P(('fsdp', 'seq'))
The draws below stay inside these ranges and needn't reach their ends.
Inputs may be any that keep to these rules, and one draw needn't show every extreme that they name: `text_len`: the number of the text slots of a sequence that are real; the others are padding. `batch_valid`: 1 marks a micro-batch of a group whose sequences count, 0 one whose sequences are padding.
All inputs are finite; a program needn't handle non-finite values.
Results may differ from the reference program's by a relative error of at most 0.014.
Values may be sent and summed in bfloat16 or wider, within the bound.
No kernel may reach another device: no remote copies, remote signals or barrier semaphores. Data moves between devices by JAX's collectives and lax.ppermute only.
A program may use at most 192 MiB of HBM per device.

```python
import jax
import jax.numpy as jnp
from jax import lax

D = 512
HEAD_DIM = 64
FF = 2048
PATCHES = 1024
TEXT = 79
MICRO = 4
SEQ_MB = 1
LENGTH = 1104
SEQS = 64
N_FSDP = 16


def draw_text_len(key, part):
    lengths = jax.random.randint(jax.random.fold_in(key, 11), (SEQS,), 1, TEXT + 1)
    lengths = lengths.at[0].set(TEXT)
    return lengths.at[SEQS - 1].set(1).astype(jnp.int32)


def with_ends(values, own_key, smallest, top_value):
    spot = [jax.random.randint(jax.random.fold_in(own_key, axis), (), 0, length) for axis, length in enumerate(values.shape)]
    widest = values.shape.index(max(values.shape))
    next_to = spot[:widest] + [(spot[widest] + 1) % values.shape[widest]] + spot[widest + 1:]
    return values.at[tuple(spot)].set(smallest).at[tuple(next_to)].set(top_value)


def block_scale(rng, dims, split, low, largest):
    level = 1.0
    for axis_at, blocks in split:
        heights = jax.random.uniform(jax.random.fold_in(jax.random.fold_in(rng, 6), axis_at), (blocks,), jnp.float32, low / len(split), largest / len(split))
        level = level * jnp.repeat(jnp.exp(heights), dims[axis_at] // blocks).reshape((-1,) + (1,) * (len(dims) - 1 - axis_at))
    return level


def gaussian(own_key, extent, scale, reach, pieces=(), held_as=jnp.bfloat16):
    array = scale * jax.random.normal(own_key, extent, jnp.float32)
    if pieces:
        array = array * block_scale(own_key, extent, pieces, -0.22, 0.18)
    return jnp.clip(array, -reach, reach).astype(held_as)


def setup_inputs(seed: int = 0) -> dict:
    key_list = jax.random.split(jax.random.key(seed), 19)
    inputs = gaussian(key_list[0], (SEQS, LENGTH, D), 1.0, 6.0, ((0, 16), (1, 2)))
    skip_input = gaussian(key_list[1], (SEQS, LENGTH, D), 1.0, 6.0, ((0, 16), (1, 2)))
    cotangent = gaussian(key_list[2], (SEQS, LENGTH, D), 1.0, 6.0, ((0, 16), (1, 2)))
    text_len = draw_text_len(jax.random.fold_in(key_list[18], 71), 0)
    batch_valid = with_ends((jax.random.randint(key_list[4], (N_FSDP, MICRO), 0, 4) < 3).astype(jnp.int32), jax.random.fold_in(key_list[4], 1), 0, 1)
    skip_weight = gaussian(key_list[5], (2 * D, D), (2 * D) ** -0.5, 0.1875, ((0, 32),))
    skip_bias = gaussian(key_list[6], (D,), 0.5, 3.0, ((0, 32),))
    first_gain = jnp.clip(1.0 + 0.18 * jax.random.normal(key_list[7], (D,), jnp.float32), 0.099609375, 1.8984375).astype(jnp.bfloat16)
    first_shift = gaussian(key_list[8], (D,), 0.5, 3.0, ((0, 32),))
    qkv_weight = gaussian(key_list[9], (D, 3 * D), D ** -0.5, 0.25, ((0, 32),))
    proj_weight = gaussian(key_list[10], (D, D), 4 ** -0.5, 3.0, ((0, 32),))
    proj_bias = gaussian(key_list[11], (D,), 0.5, 3.0, ((0, 32),))
    second_gain = jnp.clip(1.0 + 0.18 * jax.random.normal(key_list[12], (D,), jnp.float32), 0.099609375, 1.8984375).astype(jnp.bfloat16)
    second_shift = gaussian(key_list[13], (D,), 0.5, 3.0, ((0, 32),))
    up_weight = gaussian(key_list[14], (D, FF), D ** -0.5, 0.25, ((0, 32),))
    up_bias = gaussian(key_list[15], (FF,), 0.5, 3.0, ((0, 32),))
    down_weight = gaussian(key_list[16], (FF, D), FF ** -0.5, 0.125, ((0, 32),))
    down_bias = gaussian(key_list[17], (D,), 0.5, 3.0, ((0, 32),))
    return {"inputs": inputs, "skip_input": skip_input, "cotangent": cotangent, "text_len": text_len, "batch_valid": batch_valid, "skip_weight": skip_weight, "skip_bias": skip_bias, "first_gain": first_gain, "first_shift": first_shift, "qkv_weight": qkv_weight, "proj_weight": proj_weight, "proj_bias": proj_bias, "second_gain": second_gain, "second_shift": second_shift, "up_weight": up_weight, "up_bias": up_bias, "down_weight": down_weight, "down_bias": down_bias}


NEG_BIG = -1e+30
EPSILON = 1e-05

@jax.custom_vjp
def low(v):
    return lax.optimization_barrier(v.astype(jnp.bfloat16)).astype(jnp.float32)

@jax.custom_vjp
def low_back(v):
    return v

def low_keep(v):
    return (low(v), None)

def low_pass(kept, grad):
    return (grad,)

def back_keep(v):
    return (v, None)

def back_low(kept, grad):
    return (low(grad),)
low.defvjp(low_keep, low_pass)
low_back.defvjp(back_keep, back_low)

def matmul(left, right):
    return jnp.dot(left, right, precision=lax.Precision.HIGHEST, preferred_element_type=jnp.float32)

def normalize(hidden, gain, shift):
    average = lax.optimization_barrier(jnp.mean(hidden, axis=-1, keepdims=True))
    centred = hidden - average
    spread = lax.optimization_barrier(jnp.mean(centred * centred, axis=-1, keepdims=True))
    return centred * lax.rsqrt(spread + EPSILON) * gain + shift

def gelu_exact(value):
    return jax.nn.gelu(value, approximate=False)

def one_sequence(seq_in, seq_skip, params, seq_text, seq_valid):
    skip_weight, skip_bias, first_gain, first_shift, qkv_weight, proj_weight, proj_bias, second_gain, second_shift, up_weight, up_bias, down_weight, down_bias = params
    length, model_width = seq_in.shape
    head_count = model_width // HEAD_DIM
    joined = jnp.concatenate([seq_in, seq_skip], axis=1)
    stream_first = low_back(matmul(joined, skip_weight) + skip_bias)
    attn_in = low(normalize(stream_first, first_gain, first_shift))
    qkv = low_back(low(matmul(attn_in, qkv_weight)))
    queries = qkv[:, :model_width].reshape(length, head_count, HEAD_DIM)
    key_heads = qkv[:, model_width:2 * model_width].reshape(length, head_count, HEAD_DIM)
    values = qkv[:, 2 * model_width:].reshape(length, head_count, HEAD_DIM)
    scores = jnp.einsum('qhd,khd->hqk', queries, key_heads, precision=lax.Precision.HIGHEST)
    scores = low_back(scores * HEAD_DIM ** (-0.5))
    allowed = jnp.arange(length) < PATCHES + 1 + seq_text
    scores = jnp.where(allowed[None, None, :], scores, NEG_BIG)
    row_max = lax.optimization_barrier(jnp.max(scores, axis=-1, keepdims=True))
    exponent = jnp.exp(scores - row_max)
    softened = low(exponent / lax.optimization_barrier(jnp.sum(exponent, axis=-1, keepdims=True)))
    mixture = jnp.einsum('hqk,khd->qhd', softened, values, precision=lax.Precision.HIGHEST)
    mixture = low_back(low(mixture.reshape(length, model_width)))
    stream_second = stream_first + low_back(matmul(mixture, proj_weight) + proj_bias)
    mlp_in = low(normalize(stream_second, second_gain, second_shift))
    hidden_pre = low_back(matmul(mlp_in, up_weight) + up_bias)
    activated = low(gelu_exact(hidden_pre))
    branch = low_back(matmul(activated, down_weight) + down_bias)
    return (stream_second + branch) * seq_valid

def reference(inputs, skip_input, cotangent, text_len, batch_valid, skip_weight, skip_bias, first_gain, first_shift, qkv_weight, proj_weight, proj_bias, second_gain, second_shift, up_weight, up_bias, down_weight, down_bias):
    params = tuple((member.astype(jnp.float32) for member in (skip_weight, skip_bias, first_gain, first_shift, qkv_weight, proj_weight, proj_bias, second_gain, second_shift, up_weight, up_bias, down_weight, down_bias)))
    per_seq_valid = jnp.repeat(batch_valid.reshape(-1), SEQ_MB).astype(jnp.float32)

    def per_sequence(totals, sliced):
        seq_in, seq_skip, seq_cot, seq_text, seq_valid = sliced

        def forward(first_arg, second_arg, weights):
            return one_sequence(first_arg, second_arg, weights, seq_text, seq_valid)
        result, pullback = jax.vjp(forward, seq_in.astype(jnp.float32), seq_skip.astype(jnp.float32), params)
        grad_in, grad_skip, grad_params = pullback(seq_cot.astype(jnp.float32))
        totals = jax.tree.map(jnp.add, totals, grad_params)
        return (totals, (result.astype(jnp.bfloat16), grad_in.astype(jnp.bfloat16), grad_skip.astype(jnp.bfloat16)))
    initial = jax.tree.map(jnp.zeros_like, params)
    totals, stacked = lax.scan(per_sequence, initial, (inputs, skip_input, cotangent, text_len, per_seq_valid))
    output, input_grad, skip_grad = stacked
    return (output, input_grad, skip_grad, totals[0], totals[1], totals[2], totals[3], totals[4], totals[5], totals[6], totals[7], totals[8], totals[9], totals[10], totals[11], totals[12])
```

```python
import functools

import jax
import jax.numpy as jnp
from jax import lax
from jax.experimental import pallas as pl
from jax.experimental.pallas import tpu as pltpu
from jax.sharding import PartitionSpec as P

HEAD_DIM = 64
PATCHES = 1024
MICRO = 4


NEG_BIG = -1e30
EPSILON = 1e-05
heads_per_group = 4


def row_contract(left, right):
    return lax.dot_general(
        left, right, (((0,), (0,)), ((), ())), preferred_element_type=jnp.float32
    )


def column_contract(left, right):
    return lax.dot_general(
        left, right, (((1,), (1,)), ((), ())), preferred_element_type=jnp.float32
    )


def normalize(hidden, gain, shift):
    average = jnp.mean(hidden, axis=-1, keepdims=True)
    centred = hidden - average
    spread = jnp.mean(centred * centred, axis=-1, keepdims=True)
    return centred * lax.rsqrt(spread + EPSILON) * gain + shift


def gelu_exact(value):
    return jax.nn.gelu(value, approximate=False)


def head_slice(array, head_group):
    group_width = heads_per_group * HEAD_DIM
    part = lax.dynamic_slice_in_dim(array, head_group * group_width, group_width, 2)
    return part.reshape(array.shape[0], array.shape[1], heads_per_group, HEAD_DIM)


def restack(stacked):
    seq_count, length = (stacked.shape[1], stacked.shape[2])
    return jnp.transpose(stacked, (1, 2, 0, 3)).reshape(
        seq_count, length, stacked.shape[0] * stacked.shape[3]
    )


def stats_to_rows(stats):
    groups, seq_count, head_count, length = stats.shape
    return jnp.transpose(stats, (1, 3, 0, 2)).reshape(seq_count, length, groups * head_count)


def rows_to_stats(rows, groups):
    seq_count, length = (rows.shape[0], rows.shape[1])
    return jnp.transpose(rows.reshape(seq_count, length, groups, heads_per_group), (2, 0, 3, 1))


def masked_scores(query_part, key_part, allowed, score_scale):
    scores = (
        jnp.einsum("sqhd,skhd->shqk", query_part, key_part, preferred_element_type=jnp.float32)
        * score_scale
    )
    return jnp.where(allowed[:, None, None, :], scores, NEG_BIG)


def attend_forward(queries, keys_all, values_all, allowed, score_scale):
    groups = queries.shape[2] // (heads_per_group * HEAD_DIM)

    def one_group(head_group):
        query_part = head_slice(queries, head_group)
        key_part = head_slice(keys_all, head_group)
        value_part = head_slice(values_all, head_group)
        scores = masked_scores(query_part, key_part, allowed, score_scale)
        row_max = jnp.max(scores, axis=-1, keepdims=True)
        exponent = jnp.exp(scores - row_max)
        row_total = jnp.sum(exponent, axis=-1, keepdims=True)
        softened = (exponent / row_total).astype(jnp.bfloat16)
        mixture = jnp.einsum(
            "shqk,skhd->sqhd", softened, value_part, preferred_element_type=jnp.float32
        )
        logsum = (row_max + jnp.log(row_total))[..., 0]
        return (
            mixture.reshape(mixture.shape[0], mixture.shape[1], heads_per_group * HEAD_DIM),
            logsum,
        )

    mixtures, logsums = lax.map(one_group, jnp.arange(groups))
    return (restack(mixtures), logsums)


def attend_query_side(queries, keys_all, values_all, grad_mixture, logsums, allowed, score_scale):
    groups = queries.shape[2] // (heads_per_group * HEAD_DIM)

    def one_group(sliced):
        head_group, logsum = sliced
        query_part = head_slice(queries, head_group)
        key_part = head_slice(keys_all, head_group)
        value_part = head_slice(values_all, head_group)
        grad_part = head_slice(grad_mixture, head_group)
        scores = masked_scores(query_part, key_part, allowed, score_scale)
        softened = jnp.exp(scores - logsum[..., None])
        prob_grad = jnp.einsum(
            "sqhd,skhd->shqk", grad_part, value_part, preferred_element_type=jnp.float32
        )
        row_inner = jnp.sum(prob_grad * softened, axis=-1, keepdims=True)
        score_grad = (softened * (prob_grad - row_inner)).astype(jnp.bfloat16)
        query_grad = (
            jnp.einsum("shqk,skhd->sqhd", score_grad, key_part, preferred_element_type=jnp.float32)
            * score_scale
        )
        group_width = heads_per_group * HEAD_DIM
        return (
            query_grad.reshape(query_grad.shape[0], query_grad.shape[1], group_width),
            row_inner[..., 0],
        )

    query_grads, inners = lax.map(one_group, (jnp.arange(groups), logsums))
    return (restack(query_grads), inners)


def attend_key_side(
    queries_all,
    keys_here,
    values_here,
    grad_all,
    logsums_all,
    inners_all,
    allowed_here,
    score_scale,
):
    groups = keys_here.shape[2] // (heads_per_group * HEAD_DIM)

    def one_group(sliced):
        head_group, logsum, inner = sliced
        query_part = head_slice(queries_all, head_group)
        key_part = head_slice(keys_here, head_group)
        value_part = head_slice(values_here, head_group)
        grad_part = head_slice(grad_all, head_group)
        scores = masked_scores(query_part, key_part, allowed_here, score_scale)
        softened = jnp.exp(scores - logsum[..., None])
        softened_low = softened.astype(jnp.bfloat16)
        value_grad = jnp.einsum(
            "shqk,sqhd->skhd", softened_low, grad_part, preferred_element_type=jnp.float32
        )
        prob_grad = jnp.einsum(
            "sqhd,skhd->shqk", grad_part, value_part, preferred_element_type=jnp.float32
        )
        score_grad = (softened * (prob_grad - inner[..., None])).astype(jnp.bfloat16)
        key_grad = (
            jnp.einsum(
                "shqk,sqhd->skhd", score_grad, query_part, preferred_element_type=jnp.float32
            )
            * score_scale
        )
        group_width = heads_per_group * HEAD_DIM
        return (
            key_grad.reshape(key_grad.shape[0], key_grad.shape[1], group_width),
            value_grad.reshape(value_grad.shape[0], value_grad.shape[1], group_width),
        )

    key_grads, value_grads = lax.map(one_group, (jnp.arange(groups), logsums_all, inners_all))
    return (restack(key_grads), restack(value_grads))


def general(
    inputs,
    skip_input,
    cotangent,
    text_len,
    batch_valid,
    skip_weight,
    skip_bias,
    first_gain,
    first_shift,
    qkv_weight,
    proj_weight,
    proj_bias,
    second_gain,
    second_shift,
    up_weight,
    up_bias,
    down_weight,
    down_bias,
):
    local_length = inputs.shape[1]
    model_width = inputs.shape[2]
    full_length = local_length * lax.axis_size("seq")
    per_batch = inputs.shape[0] // MICRO
    rows_here = per_batch * local_length
    score_scale = HEAD_DIM ** (-0.5)
    groups = model_width // (heads_per_group * HEAD_DIM)
    key_position = jnp.arange(full_length, dtype=jnp.int32)
    local_position = lax.axis_index("seq") * local_length + jnp.arange(
        local_length, dtype=jnp.int32
    )
    totals = None
    outputs, input_grads, skip_grads = ([], [], [])
    for micro_batch in range(MICRO):
        first_row = micro_batch * per_batch
        last_row = first_row + per_batch
        params = (
            lax.all_gather(skip_weight, ("fsdp", "seq"), axis=0, tiled=True),
            lax.all_gather(skip_bias, ("fsdp", "seq"), axis=0, tiled=True),
            lax.all_gather(first_gain, ("fsdp", "seq"), axis=0, tiled=True),
            lax.all_gather(first_shift, ("fsdp", "seq"), axis=0, tiled=True),
            lax.all_gather(qkv_weight, ("fsdp", "seq"), axis=0, tiled=True),
            lax.all_gather(proj_weight, ("fsdp", "seq"), axis=0, tiled=True),
            lax.all_gather(proj_bias, ("fsdp", "seq"), axis=0, tiled=True),
            lax.all_gather(second_gain, ("fsdp", "seq"), axis=0, tiled=True),
            lax.all_gather(second_shift, ("fsdp", "seq"), axis=0, tiled=True),
            lax.all_gather(up_weight, ("fsdp", "seq"), axis=0, tiled=True),
            lax.all_gather(up_bias, ("fsdp", "seq"), axis=0, tiled=True),
            lax.all_gather(down_weight, ("fsdp", "seq"), axis=0, tiled=True),
            lax.all_gather(down_bias, ("fsdp", "seq"), axis=0, tiled=True),
        )
        (
            skip_matrix,
            skip_offset,
            gain_one,
            shift_one,
            qkv_matrix,
            proj_matrix,
            proj_offset,
            gain_two,
            shift_two,
            up_matrix,
            up_offset,
            down_matrix,
            down_offset,
        ) = params
        joined = jnp.concatenate(
            [inputs[first_row:last_row], skip_input[first_row:last_row]], axis=2
        ).reshape(rows_here, 2 * model_width)
        stream_first = jnp.dot(
            joined, skip_matrix, preferred_element_type=jnp.float32
        ) + skip_offset.astype(jnp.float32)
        normed_first, back_first = jax.vjp(
            normalize, stream_first, gain_one.astype(jnp.float32), shift_one.astype(jnp.float32)
        )
        attn_in = normed_first.astype(jnp.bfloat16)
        qkv_low = jnp.dot(attn_in, qkv_matrix, preferred_element_type=jnp.float32).astype(
            jnp.bfloat16
        )
        qkv_low = qkv_low.reshape(per_batch, local_length, 3 * model_width)
        queries = qkv_low[..., :model_width]
        keys_here = qkv_low[..., model_width : 2 * model_width]
        values_here = qkv_low[..., 2 * model_width :]
        keys_all, values_all = (
            lax.all_gather(keys_here, "seq", axis=1, tiled=True),
            lax.all_gather(values_here, "seq", axis=1, tiled=True),
        )
        limits = (PATCHES + 1 + text_len[first_row:last_row])[:, None]
        allowed = key_position[None, :] < limits
        mixture, logsums = attend_forward(queries, keys_all, values_all, allowed, score_scale)
        mixture_low = mixture.astype(jnp.bfloat16).reshape(rows_here, model_width)
        stream_second = (
            stream_first
            + jnp.dot(mixture_low, proj_matrix, preferred_element_type=jnp.float32)
            + proj_offset.astype(jnp.float32)
        )
        normed_second, back_second = jax.vjp(
            normalize, stream_second, gain_two.astype(jnp.float32), shift_two.astype(jnp.float32)
        )
        mlp_in = normed_second.astype(jnp.bfloat16)
        hidden_pre = jnp.dot(
            mlp_in, up_matrix, preferred_element_type=jnp.float32
        ) + up_offset.astype(jnp.float32)
        activated, back_gelu = jax.vjp(gelu_exact, hidden_pre)
        activated_low = activated.astype(jnp.bfloat16)
        branch = jnp.dot(
            activated_low, down_matrix, preferred_element_type=jnp.float32
        ) + down_offset.astype(jnp.float32)
        validity = batch_valid[0, micro_batch].astype(jnp.float32)
        outputs.append(
            ((stream_second + branch) * validity)
            .astype(jnp.bfloat16)
            .reshape(per_batch, local_length, model_width)
        )
        params = (
            lax.all_gather(skip_weight, ("fsdp", "seq"), axis=0, tiled=True),
            lax.all_gather(skip_bias, ("fsdp", "seq"), axis=0, tiled=True),
            lax.all_gather(first_gain, ("fsdp", "seq"), axis=0, tiled=True),
            lax.all_gather(first_shift, ("fsdp", "seq"), axis=0, tiled=True),
            lax.all_gather(qkv_weight, ("fsdp", "seq"), axis=0, tiled=True),
            lax.all_gather(proj_weight, ("fsdp", "seq"), axis=0, tiled=True),
            lax.all_gather(proj_bias, ("fsdp", "seq"), axis=0, tiled=True),
            lax.all_gather(second_gain, ("fsdp", "seq"), axis=0, tiled=True),
            lax.all_gather(second_shift, ("fsdp", "seq"), axis=0, tiled=True),
            lax.all_gather(up_weight, ("fsdp", "seq"), axis=0, tiled=True),
            lax.all_gather(up_bias, ("fsdp", "seq"), axis=0, tiled=True),
            lax.all_gather(down_weight, ("fsdp", "seq"), axis=0, tiled=True),
            lax.all_gather(down_bias, ("fsdp", "seq"), axis=0, tiled=True),
        )
        (
            skip_matrix,
            skip_offset,
            gain_one,
            shift_one,
            qkv_matrix,
            proj_matrix,
            proj_offset,
            gain_two,
            shift_two,
            up_matrix,
            up_offset,
            down_matrix,
            down_offset,
        ) = params
        grad_out = (
            cotangent[first_row:last_row].reshape(rows_here, model_width).astype(jnp.float32)
            * validity
        )
        grad_branch = grad_out.astype(jnp.bfloat16)
        down_grad = row_contract(activated_low, grad_branch)
        down_offset_grad = jnp.sum(grad_branch.astype(jnp.float32), axis=0)
        grad_act = column_contract(grad_branch, down_matrix)
        (grad_pre,) = back_gelu(grad_act)
        grad_pre_low = grad_pre.astype(jnp.bfloat16)
        up_grad = row_contract(mlp_in, grad_pre_low)
        up_offset_grad = jnp.sum(grad_pre_low.astype(jnp.float32), axis=0)
        grad_mlp_in = column_contract(grad_pre_low, up_matrix)
        norm_term_second, gain_two_grad, shift_two_grad = back_second(grad_mlp_in)
        grad_stream_second = grad_out + norm_term_second
        grad_proj = grad_stream_second.astype(jnp.bfloat16)
        proj_grad = row_contract(mixture_low, grad_proj)
        proj_offset_grad = jnp.sum(grad_proj.astype(jnp.float32), axis=0)
        grad_mixture = (
            column_contract(grad_proj, proj_matrix)
            .astype(jnp.bfloat16)
            .reshape(per_batch, local_length, model_width)
        )
        query_grad, inners = attend_query_side(
            queries, keys_all, values_all, grad_mixture, logsums, allowed, score_scale
        )
        queries_all, grad_all = (
            lax.all_gather(queries, "seq", axis=1, tiled=True),
            lax.all_gather(grad_mixture, "seq", axis=1, tiled=True),
        )
        logsum_rows, inner_rows = (
            lax.all_gather(stats_to_rows(logsums), "seq", axis=1, tiled=True),
            lax.all_gather(stats_to_rows(inners), "seq", axis=1, tiled=True),
        )
        allowed_here = local_position[None, :] < limits
        key_grad, value_grad = attend_key_side(
            queries_all,
            keys_here,
            values_here,
            grad_all,
            rows_to_stats(logsum_rows, groups),
            rows_to_stats(inner_rows, groups),
            allowed_here,
            score_scale,
        )
        grad_qkv = (
            jnp.concatenate([query_grad, key_grad, value_grad], axis=2)
            .astype(jnp.bfloat16)
            .reshape(rows_here, 3 * model_width)
        )
        qkv_grad = row_contract(attn_in, grad_qkv)
        grad_attn_in = column_contract(grad_qkv, qkv_matrix)
        norm_term_first, gain_one_grad, shift_one_grad = back_first(grad_attn_in)
        grad_stream_first = (grad_stream_second + norm_term_first).astype(jnp.bfloat16)
        skip_matrix_grad = row_contract(joined, grad_stream_first)
        skip_offset_grad = jnp.sum(grad_stream_first.astype(jnp.float32), axis=0)
        grad_joined = column_contract(grad_stream_first, skip_matrix).reshape(
            per_batch, local_length, 2 * model_width
        )
        input_grads.append(grad_joined[..., :model_width].astype(jnp.bfloat16))
        skip_grads.append(grad_joined[..., model_width:].astype(jnp.bfloat16))
        step_grads = (
            skip_matrix_grad,
            skip_offset_grad,
            gain_one_grad,
            shift_one_grad,
            qkv_grad,
            proj_grad,
            proj_offset_grad,
            gain_two_grad,
            shift_two_grad,
            up_grad,
            up_offset_grad,
            down_grad,
            down_offset_grad,
        )
        if totals is None:
            totals = tuple(step_grads)
        else:
            totals = jax.tree.map(jnp.add, tuple(totals), tuple(step_grads))
    totals = (
        lax.psum_scatter(totals[0], ("fsdp", "seq"), scatter_dimension=0, tiled=True),
        lax.psum_scatter(totals[1], ("fsdp", "seq"), scatter_dimension=0, tiled=True),
        lax.psum_scatter(totals[2], ("fsdp", "seq"), scatter_dimension=0, tiled=True),
        lax.psum_scatter(totals[3], ("fsdp", "seq"), scatter_dimension=0, tiled=True),
        lax.psum_scatter(totals[4], ("fsdp", "seq"), scatter_dimension=0, tiled=True),
        lax.psum_scatter(totals[5], ("fsdp", "seq"), scatter_dimension=0, tiled=True),
        lax.psum_scatter(totals[6], ("fsdp", "seq"), scatter_dimension=0, tiled=True),
        lax.psum_scatter(totals[7], ("fsdp", "seq"), scatter_dimension=0, tiled=True),
        lax.psum_scatter(totals[8], ("fsdp", "seq"), scatter_dimension=0, tiled=True),
        lax.psum_scatter(totals[9], ("fsdp", "seq"), scatter_dimension=0, tiled=True),
        lax.psum_scatter(totals[10], ("fsdp", "seq"), scatter_dimension=0, tiled=True),
        lax.psum_scatter(totals[11], ("fsdp", "seq"), scatter_dimension=0, tiled=True),
        lax.psum_scatter(totals[12], ("fsdp", "seq"), scatter_dimension=0, tiled=True),
    )
    output = jnp.concatenate(outputs, axis=0)
    input_grad = jnp.concatenate(input_grads, axis=0)
    skip_grad = jnp.concatenate(skip_grads, axis=0)
    return (
        output,
        input_grad,
        skip_grad,
        totals[0],
        totals[1],
        totals[2],
        totals[3],
        totals[4],
        totals[5],
        totals[6],
        totals[7],
        totals[8],
        totals[9],
        totals[10],
        totals[11],
        totals[12],
    )


EPS=1e-5
bf=jnp.bfloat16; f32=jnp.float32
MASKED=-1e30

def dot_nn(a,b): return lax.dot_general(a,b,(((1,),(0,)),((),())),preferred_element_type=f32)
def dot_nt(a,b): return lax.dot_general(a,b,(((1,),(1,)),((),())),preferred_element_type=f32)
def dot_tn(a,b): return lax.dot_general(a,b,(((0,),(0,)),((),())),preferred_element_type=f32)

def lane_iota(shape): return lax.broadcasted_iota(jnp.int32, shape, len(shape)-1)
def row_iota(shape): return lax.broadcasted_iota(jnp.int32, shape, len(shape)-2)

def norm_parts(h):
    mu=jnp.mean(h,axis=-1,keepdims=True)
    c=h-mu
    var=jnp.mean(c*c,axis=-1,keepdims=True)
    r=lax.rsqrt(var+EPS)
    return c*r, r

def attn_fwd_kernel(meta, sf_ref, w_ref, g_ref, b_ref, qkv_ref, e_ref, mix_ref, r_ref, qp, ot, *, L, QP, QB):
    i=pl.program_id(0)
    W=128
    @pl.when(i==0)
    def _():
        n,_=norm_parts(sf_ref[...].astype(f32))
        a=(n*g_ref[...]+b_ref[...]).astype(bf)
        for j in range(6):
            t=dot_nn(a,w_ref[:,256*j:256*(j+1)]).astype(bf)
            qkv_ref[2*j]=t[:,:128]
            qkv_ref[2*j+1]=t[:,128:]
        qp[L:,:]=jnp.zeros((QP-L,W),bf)
    lane=lane_iota((1,W))
    q=qkv_ref[i].astype(f32)*(HEAD_DIM**-0.5)
    qp[:L,:]=q.astype(bf)
    k=qkv_ref[4+i]
    vt=qkv_ref[8+i].T
    half=meta[0]; y=meta[1]; limit=meta[2]
    row=row_iota((L,W))
    pos=jnp.where(row<half, row+y*half, row-half+(1-y)*half) if True else row
    bias=jnp.where(pos<limit, 0.0, MASKED).astype(bf)
    qfull=qp[...]
    for h in range(2):
        mine=(lane>=64*h)&(lane<64*h+64)
        spare=64*(1-h)
        ka=jnp.where(mine,k,jnp.where(lane==spare,bias,jnp.zeros_like(bias)))
        qa=jnp.where(lane==spare, jnp.ones_like(qfull), qfull)
        for j in range(QP//QB):
            s=dot_nt(ka,qa[j*QB:(j+1)*QB])
            m=jnp.max(s,axis=0,keepdims=True)
            e=jnp.exp(s-m)
            t=jnp.sum(e,axis=0,keepdims=True)
            el=e.astype(bf)
            e_ref[h,:,j*QB:(j+1)*QB]=el
            r=1.0/t
            r_ref[0,h:h+1,j*QB:(j+1)*QB]=r
            ot[64*h:64*h+64,j*QB:(j+1)*QB]=dot_nn(vt[64*h:64*h+64],el)*r
    mix_ref[...]=ot[...].astype(bf).T[:L]

def attn_fwd(meta, sf, w, g, b, *, QB=384):
    L,D=sf.shape
    QP=-(-L//128)*128
    H2=D//128
    full=lambda *s: pl.BlockSpec(s, lambda i,m:(0,)*len(s))
    return pl.pallas_call(
        functools.partial(attn_fwd_kernel,L=L,QP=QP,QB=QB),
        grid_spec=pltpu.PrefetchScalarGridSpec(num_scalar_prefetch=1, grid=(H2,),
          in_specs=[full(L,D),full(D,3*D),full(1,D),full(1,D)],
          out_specs=[full(3*H2,L,128), pl.BlockSpec((2,L,QP),lambda i,m:(i,0,0)), pl.BlockSpec((L,128),lambda i,m:(0,i)), pl.BlockSpec((1,2,QP),lambda i,m:(i,0,0))],
          scratch_shapes=[pltpu.VMEM((QP,128),bf), pltpu.VMEM((128,QP),f32)]),
        out_shape=[jax.ShapeDtypeStruct((3*H2,L,128),bf), jax.ShapeDtypeStruct((2*H2,L,QP),bf), jax.ShapeDtypeStruct((L,D),bf), jax.ShapeDtypeStruct((H2,2,QP),f32)],
        compiler_params=pltpu.CompilerParams(vmem_limit_bytes=60<<20),
        name="attn_fwd",
        cost_estimate=pl.CostEstimate(flops=int(2*L*D*3*D+8*4*L*L*256), bytes_accessed=int(20e6), transcendentals=8*L*L),
    )(meta, sf, w, g, b)

def attn_bwd_kernel(q_ref,k_ref,v_ref,e_ref,o_ref,do_ref,r_ref, sf_ref, gss_ref, w_ref, g_ref, b_ref,
                    gsf_ref, gw_ref, gg_ref, gb_ref, gq, qp, dop, qt, ds, *, L, QP, QB, H2):
    i=pl.program_id(0)
    W=128
    @pl.when(i==0)
    def _():
        qp[L:,:]=jnp.zeros((QP-L,W),bf)
        dop[L:,:]=jnp.zeros((QP-L,W),f32)
    lane=lane_iota((1,W))
    qp[:L,:]=(q_ref[0].astype(f32)*(HEAD_DIM**-0.5)).astype(bf)
    do=do_ref[...].astype(f32)
    rt=jnp.concatenate([r_ref[0], jnp.zeros((6,QP),f32)],axis=0).T
    r0=rt[:L,0:1]; r1=rt[:L,1:2]
    dop[:L,:]=do*jnp.where(lane<64,r0,r1)
    dof=dop[...]
    dob=dof.astype(bf)
    o=o_ref[...].astype(f32)
    prod=o*dob[:L].astype(f32)
    qf=qp[...]
    k=k_ref[0]; v=v_ref[0]
    kt=k.T
    dv=jnp.zeros((L,W),f32); dk=jnp.zeros((L,W),f32)
    for h in range(2):
        mine=(lane>=64*h)&(lane<64*h+64)
        sp=64*(1-h)
        inner=jnp.sum(jnp.where(mine,prod,0.0),axis=1,keepdims=True)
        ihi=inner.astype(bf); ilo=(inner-ihi.astype(f32)).astype(bf)
        ihi=jnp.concatenate([ihi.astype(f32),jnp.zeros((QP-L,1),f32)],axis=0)
        ilo=jnp.concatenate([ilo.astype(f32),jnp.zeros((QP-L,1),f32)],axis=0)
        dom=jnp.where(mine,dob,jnp.zeros_like(dob))
        doa=jnp.where(mine,dob,jnp.where(lane==sp,-ihi,jnp.where(lane==sp+1,-ilo,0.0)).astype(bf))
        va=jnp.where(mine,v,jnp.where((lane==sp)|(lane==sp+1),jnp.ones_like(v),jnp.zeros_like(v)))
        dv=dv+dot_nn(e_ref[h],dom)
        for j in range(QP//QB):
            dp=dot_nt(va,doa[j*QB:(j+1)*QB])
            d=(e_ref[h,:,j*QB:(j+1)*QB].astype(f32)*dp).astype(bf)
            ds[:,j*QB:(j+1)*QB]=d
            qt[64*h:64*h+64,j*QB:(j+1)*QB]=dot_nn(kt[64*h:64*h+64],d)
        dk=dk+dot_nn(ds[...],jnp.where(mine,qf,jnp.zeros_like(qf)))
    gq[i]=(qt[...]*(HEAD_DIM**-0.5)).astype(bf).T[:L]
    gq[H2+i]=dk.astype(bf)
    gq[2*H2+i]=dv.astype(bf)
    @pl.when(i==H2-1)
    def _():
        n,r=norm_parts(sf_ref[...].astype(f32))
        a=(n*g_ref[...]+b_ref[...]).astype(bf)
        acc=jnp.zeros(n.shape,f32)
        for j in range(3*H2//2):
            t=jnp.concatenate([gq[2*j],gq[2*j+1]],axis=1)
            acc=acc+dot_nt(t,w_ref[:,256*j:256*(j+1)])
            gw_ref[:,256*j:256*(j+1)]=dot_tn(a,t)
        gg_ref[...]=jnp.sum(acc*n,axis=0,keepdims=True)
        gb_ref[...]=jnp.sum(acc,axis=0,keepdims=True)
        e=acc*g_ref[...]
        gs=gss_ref[...]+r*(e-jnp.mean(e,axis=1,keepdims=True)-n*jnp.mean(e*n,axis=1,keepdims=True))
        gsf_ref[...]=gs.astype(bf)

def attn_bwd(qkv,e,mix,dmix,r,sf,gss,w,g,b,*,QB=384):
    L,D=sf.shape
    H2=D//128
    QP=e.shape[2]
    full=lambda *s: pl.BlockSpec(s, lambda i:(0,)*len(s))
    col=pl.BlockSpec((L,128),lambda i:(0,i))
    return pl.pallas_call(
        functools.partial(attn_bwd_kernel,L=L,QP=QP,QB=QB,H2=H2),
        grid=(H2,),
        in_specs=[pl.BlockSpec((1,L,128),lambda i:(i,0,0)),pl.BlockSpec((1,L,128),lambda i:(H2+i,0,0)),pl.BlockSpec((1,L,128),lambda i:(2*H2+i,0,0)),
          pl.BlockSpec((2,L,QP),lambda i:(i,0,0)), col, col, pl.BlockSpec((1,2,QP),lambda i:(i,0,0)),
          full(L,D), full(L,D), full(D,3*D), full(1,D), full(1,D)],
        out_specs=[full(L,D),full(D,3*D),full(1,D),full(1,D)],
        out_shape=[jax.ShapeDtypeStruct((L,D),bf),jax.ShapeDtypeStruct((D,3*D),f32),jax.ShapeDtypeStruct((1,D),f32),jax.ShapeDtypeStruct((1,D),f32)],
        scratch_shapes=[pltpu.VMEM((3*H2,L,128),bf),pltpu.VMEM((QP,128),bf),pltpu.VMEM((QP,128),f32),pltpu.VMEM((128,QP),f32),pltpu.VMEM((L,QP),bf)],
        compiler_params=pltpu.CompilerParams(vmem_limit_bytes=62<<20),
        name="attn_bwd",
        cost_estimate=pl.CostEstimate(flops=int(2*2*L*D*3*D+8*8*L*L*256), bytes_accessed=int(30e6), transcendentals=0),
    )(qkv,qkv,qkv,e,mix,dmix,r,sf,gss,w,g,b)

def gelu_both(v):
    c=lax.erf(v*(0.5**0.5))
    cdf=0.5+0.5*c
    pdf=jnp.exp(-0.5*v*v)*0.3989422804014327
    return v*cdf, cdf+v*pdf

def mid_kernel(valid_ref, mix_ref, sf_ref, cot_ref, pw, pb, g2, b2, uw, ub, dw, db,
               out_ref, gmix_ref, gss_ref, gpw_ref, guw_ref, gdw_ref, gpb_ref, gg_ref, gb_ref, gub_ref, gdb_ref,
               apw, auw, adw, *, T, L, FC):
    i=pl.program_id(0)
    @pl.when(i==0)
    def _():
        for a in (apw,auw,adw,gpb_ref,gg_ref,gb_ref,gub_ref,gdb_ref):
            a[...]=jnp.zeros(a.shape,a.dtype)
    D=mix_ref.shape[1]; F=uw.shape[1]
    mix=mix_ref[...]
    ss=sf_ref[...].astype(f32)+dot_nn(mix,pw[...])+pb[...]
    n,r=norm_parts(ss)
    mlp=(n*g2[...]+b2[...]).astype(bf)
    row=row_iota((T,1))+i*T
    valid=jnp.where(row<L, valid_ref[0], valid_ref[1]).astype(f32)
    gout=cot_ref[...].astype(f32)*valid
    gb=gout.astype(bf)
    gdb_ref[...]+=jnp.sum(gout,axis=0,keepdims=True)
    branch=jnp.zeros((T,D),f32); gm=jnp.zeros((T,D),f32)
    for c in range(F//FC):
        cs=slice(c*FC,(c+1)*FC)
        hp=dot_nn(mlp,uw[:,cs])+ub[:,cs]
        act,dact=gelu_both(hp)
        al=act.astype(bf)
        branch=branch+dot_nn(al,dw[cs,:])
        adw[cs,:]+=dot_tn(al,gb)
        gp=dot_nt(gb,dw[cs,:])*dact
        gl=gp.astype(bf)
        gub_ref[:,cs]+=jnp.sum(gl.astype(f32),axis=0,keepdims=True)
        auw[:,cs]+=dot_tn(mlp,gl)
        gm=gm+dot_nt(gl,uw[:,cs])
    out_ref[...]=((ss+branch+db[...])*valid).astype(bf)
    gg_ref[...]+=jnp.sum(gm*n,axis=0,keepdims=True)
    gb_ref[...]+=jnp.sum(gm,axis=0,keepdims=True)
    e=gm*g2[...]
    gs=gout+r*(e-jnp.mean(e,axis=1,keepdims=True)-n*jnp.mean(e*n,axis=1,keepdims=True))
    gss_ref[...]=gs
    gl=gs.astype(bf)
    gpb_ref[...]+=jnp.sum(gl.astype(f32),axis=0,keepdims=True)
    apw[...]+=dot_tn(mix,gl)
    gmix_ref[...]=dot_nt(gl,pw[...]).astype(bf)
    @pl.when(i==pl.num_programs(0)-1)
    def _():
        gpw_ref[...]=apw[...].astype(gpw_ref.dtype)
        guw_ref[...]=auw[...].astype(guw_ref.dtype)
        gdw_ref[...]=adw[...].astype(gdw_ref.dtype)

def mid(valid, mix, sf, cot, pw, pb, g2, b2, uw, ub, dw, db, *, L, T, FC=512, gdt=bf):
    N,D=mix.shape; F=uw.shape[1]
    tile=pl.BlockSpec((T,D),lambda i,m:(i,0))
    full=lambda *s: pl.BlockSpec(s, lambda i,m:(0,)*len(s), pipeline_mode=pl.Buffered(1))
    sd=jax.ShapeDtypeStruct
    return pl.pallas_call(
        functools.partial(mid_kernel,T=T,L=L,FC=FC),
        grid_spec=pltpu.PrefetchScalarGridSpec(num_scalar_prefetch=1,grid=(N//T,),
          in_specs=[tile,tile,tile,full(D,D),full(1,D),full(1,D),full(1,D),full(D,F),full(1,F),full(F,D),full(1,D)],
          out_specs=[tile,tile,tile,full(D,D),full(D,F),full(F,D),full(1,D),full(1,D),full(1,D),full(1,F),full(1,D)],
          scratch_shapes=[pltpu.VMEM((D,D),f32),pltpu.VMEM((D,F),f32),pltpu.VMEM((F,D),f32)]),
        out_shape=[sd((N,D),bf),sd((N,D),bf),sd((N,D),f32),sd((D,D),gdt),sd((D,F),gdt),sd((F,D),gdt),
                   sd((1,D),f32),sd((1,D),f32),sd((1,D),f32),sd((1,F),f32),sd((1,D),f32)],
        compiler_params=pltpu.CompilerParams(vmem_limit_bytes=62<<20),
        name="mid",
        cost_estimate=pl.CostEstimate(flops=int(3*2*N*(D*D+2*D*F)), bytes_accessed=int(25e6), transcendentals=2*N*F),
    )(valid,mix,sf,cot,pw,pb,g2,b2,uw,ub,dw,db)


BOTH = ("fsdp", "seq")
SWAP = ((0, 1), (1, 0))


def pack_rows(arrays, width):
    vectors = jnp.concatenate([a.reshape(-1) for a in arrays if a.ndim == 1])
    space = (-vectors.shape[0]) % (16 * width)
    rows = [a.reshape(-1, width) for a in arrays if a.ndim == 2]
    rows.append(jnp.pad(vectors, (0, space)).reshape(-1, width))
    return jnp.concatenate(rows, axis=0)


def unpack_rows(packed, arrays, width):
    devices = packed.shape[0]
    found, at = {}, 0
    for index, a in enumerate(arrays):
        if a.ndim == 2:
            rows = a.size // width
            piece = packed[:, at : at + rows]
            found[index] = piece.reshape(devices * a.shape[0], a.shape[1])
            at += rows
    vectors = packed[:, at:].reshape(devices, -1)
    at = 0
    for index, a in enumerate(arrays):
        if a.ndim == 1:
            found[index] = vectors[:, at : at + a.size].reshape(-1)
            at += a.size
    return [found[index] for index in range(len(arrays))]


def pack_grads(grads, arrays, width):
    devices = grads[0].shape[0] // arrays[0].shape[0]
    rows = []
    for g, a in zip(grads, arrays):
        if a.ndim == 2:
            rows.append(g.astype(bf).reshape(devices, -1, width))
    vectors = jnp.concatenate(
        [g.reshape(devices, -1) for g, a in zip(grads, arrays) if a.ndim == 1], axis=1
    ).astype(bf)
    space = (-vectors.shape[1]) % (16 * width)
    rows.append(jnp.pad(vectors, ((0, 0), (0, space))).reshape(devices, -1, width))
    return jnp.concatenate(rows, axis=1)


def paired(inputs, skip_input, cotangent, text_len, batch_valid, *params):
    half, width = inputs.shape[1:]
    length = 2 * half
    side = lax.axis_index("seq")
    held = inputs.shape[0] // 2
    swap = lambda a: lax.ppermute(a, "seq", SWAP)
    keep = lambda a: lax.dynamic_slice_in_dim(a, side * held, held, 0)
    give = lambda a: lax.dynamic_slice_in_dim(a, (1 - side) * held, held, 0)

    packed = pack_rows(params, width)
    gathered = lax.all_gather(packed, BOTH, axis=0)
    (
        skip_matrix,
        skip_offset,
        gain_one,
        shift_one,
        qkv_matrix,
        proj_matrix,
        proj_offset,
        gain_two,
        shift_two,
        up_matrix,
        up_offset,
        down_matrix,
        down_offset,
    ) = unpack_rows(gathered, params, width)
    row = lambda v: v.astype(f32)[None, :]

    def first_stream(x, s):
        return (
            jnp.dot(x, skip_matrix[:width], preferred_element_type=f32)
            + jnp.dot(s, skip_matrix[width:], preferred_element_type=f32)
            + skip_offset.astype(f32)
        ).astype(bf)

    cot_there = swap(give(cotangent))
    stream_there = swap(first_stream(give(inputs), give(skip_input)))
    stream_here = first_stream(keep(inputs), keep(skip_input))
    stream = jnp.concatenate([stream_here, stream_there], axis=1)
    cot = jnp.concatenate([keep(cotangent), cot_there], axis=1)
    lens = keep(text_len)
    valid = lax.dynamic_slice_in_dim(batch_valid[0], side * held, held, 0)

    fwd = []
    for s in range(held):
        meta = jnp.stack([jnp.int32(half), side.astype(jnp.int32), PATCHES + 1 + lens[s]])
        fwd.append(attn_fwd(meta, stream[s], qkv_matrix, row(gain_one), row(shift_one)))
    mix = jnp.concatenate([f[2] for f in fwd], axis=0)
    (
        out,
        grad_mix,
        grad_second,
        proj_grad,
        up_grad,
        down_grad,
        proj_offset_grad,
        gain_two_grad,
        shift_two_grad,
        up_offset_grad,
        down_offset_grad,
    ) = mid(
        valid,
        mix,
        stream.reshape(-1, width),
        cot.reshape(-1, width),
        proj_matrix,
        row(proj_offset),
        row(gain_two),
        row(shift_two),
        up_matrix,
        row(up_offset),
        down_matrix,
        row(down_offset),
        L=length,
        T=736,
    )
    out = out.reshape(held, length, width)
    grad_mix = grad_mix.reshape(held, length, width)
    grad_second = grad_second.reshape(held, length, width)
    out_there = swap(out[:, half:])
    bwd = []
    for s in range(held):
        qkv, e, m, r = fwd[s]
        bwd.append(
            attn_bwd(
                qkv, e, m, grad_mix[s], r, stream[s], grad_second[s], qkv_matrix, row(gain_one), row(shift_one)
            )
        )
    total = lambda k: functools.reduce(jnp.add, [b[k] for b in bwd])
    grad_first = jnp.stack([b[0] for b in bwd])
    first_here = grad_first[:, :half]
    first_there = swap(grad_first[:, half:])

    def own_order(here, there):
        low = jnp.where(side == 0, here, there)
        high = jnp.where(side == 0, there, here)
        return jnp.concatenate([low, high], axis=0)

    output = own_order(out[:, :half], out_there)
    first = own_order(first_here, first_there)
    flat = first.reshape(-1, width)
    input_grad = dot_nt(flat, skip_matrix[:width]).astype(bf).reshape(inputs.shape)
    skip_grad = dot_nt(flat, skip_matrix[width:]).astype(bf).reshape(inputs.shape)
    skip_matrix_grad = jnp.concatenate(
        [dot_tn(inputs.reshape(-1, width), flat), dot_tn(skip_input.reshape(-1, width), flat)], axis=0
    )
    skip_offset_grad = jnp.sum(flat.astype(f32), axis=0)
    grads = [
        skip_matrix_grad,
        skip_offset_grad,
        total(2)[0],
        total(3)[0],
        total(1),
        proj_grad,
        proj_offset_grad[0],
        gain_two_grad[0],
        shift_two_grad[0],
        up_grad,
        up_offset_grad[0],
        down_grad,
        down_offset_grad[0],
    ]
    scattered = lax.psum_scatter(pack_grads(grads, params, width), BOTH, scatter_dimension=0)
    own = unpack_rows(scattered[None], params, width)
    return (output, input_grad, skip_grad, *[g.astype(f32) for g in own])


def body_for(mesh):
    return paired if mesh.shape["seq"] == 2 else general


def solution(mesh):
    return jax.shard_map(
        body_for(mesh),
        mesh=mesh,
        in_specs=(
            P("fsdp", "seq", None),
            P("fsdp", "seq", None),
            P("fsdp", "seq", None),
            P("fsdp"),
            P("fsdp", None),
            P(("fsdp", "seq"), None),
            P(("fsdp", "seq")),
            P(("fsdp", "seq")),
            P(("fsdp", "seq")),
            P(("fsdp", "seq"), None),
            P(("fsdp", "seq"), None),
            P(("fsdp", "seq")),
            P(("fsdp", "seq")),
            P(("fsdp", "seq")),
            P(("fsdp", "seq"), None),
            P(("fsdp", "seq")),
            P(("fsdp", "seq"), None),
            P(("fsdp", "seq")),
        ),
        out_specs=(
            P("fsdp", "seq", None),
            P("fsdp", "seq", None),
            P("fsdp", "seq", None),
            P(("fsdp", "seq"), None),
            P(("fsdp", "seq")),
            P(("fsdp", "seq")),
            P(("fsdp", "seq")),
            P(("fsdp", "seq"), None),
            P(("fsdp", "seq"), None),
            P(("fsdp", "seq")),
            P(("fsdp", "seq")),
            P(("fsdp", "seq")),
            P(("fsdp", "seq"), None),
            P(("fsdp", "seq")),
            P(("fsdp", "seq"), None),
            P(("fsdp", "seq")),
        ),
        check_vma=False,
    )
```
